128 devices in a mesh: rows: 16 (over y, z), rep: 8 (over x, core).
Axes of the slice: x: 4, y: 4, z: 4, core: 2. Of those that a mesh axis runs over, the one named last changes fastest.
Arguments:
- features: bfloat16 [65536, 128], P('rows'), may hold values from -6 to 6
- tile_values: bfloat16 [16, 8, 512, 128, 128], P('rows', 'rep'), may hold values from -0.1875 to 0.1875
- tile_rows: int32 [16, 8, 512], P('rows', 'rep'), may hold values from 0 to 31
- tile_slots: int32 [16, 8, 512], P('rows', 'rep'), may hold values from 0 to 127
- tile_counts: int32 [16, 8], P('rows', 'rep'), may hold values from 64 to 512, as said below
- fetch_lists: int32 [16, 16, 8], P('rows'), may hold values from 0 to 31, as said below
- filter_weights: bfloat16 [4, 128, 256], replicated, may hold values from -0.5 to 0.5
Outputs:
- convolved: bfloat16 [65536, 256], P(('rows', 'rep'))
The draws below stay inside these ranges and needn't reach their ends.
Inputs may be any that keep to these rules, and one draw needn't show every extreme that they name: Tile slots from tile_counts[r, j] on carry no part of the operator; one device has all 512 slots live. `fetch_lists`: the 8 entries of one reader and one owner are distinct.
All inputs are finite; a program needn't handle non-finite values.
Results may differ from the reference program's by a relative error of at most 0.0065.
Values may be sent and summed in bfloat16 or wider, within the bound.
No kernel may reach another device: no remote copies, remote signals or barrier semaphores. Data moves between devices by JAX's collectives and lax.ppermute only.
A program may use at most 128 MiB of HBM per device.

```python
import jax
import jax.numpy as jnp
from jax import lax

F_IN = 128
F_OUT = 256
TILE = 128
DEGREE = 3
RB = 32
PER_PEER = 8
TMAX = 512
SLOTS = 128
NODES = 65536
N_ROWS = 16
N_REP = 8


def draw_tile_counts(key, part):
    base = jax.random.randint(key, (N_ROWS * N_REP,), TMAX // 8, TMAX // 2, dtype=jnp.int32)
    chosen = jax.random.randint(jax.random.fold_in(key, 1), (), 0, N_ROWS * N_REP, dtype=jnp.int32)
    filled = jnp.where(jnp.arange(N_ROWS * N_REP, dtype=jnp.int32) == chosen, TMAX, base)
    return filled.reshape(N_ROWS, N_REP).astype(jnp.int32)


def draw_fetch_lists(key, part):
    scores = jax.random.randint(key, (N_ROWS, N_ROWS, RB), 0, 1 << 20, dtype=jnp.int32)
    scores = scores * RB + jnp.arange(RB, dtype=jnp.int32)
    scores = scores.at[0, 0, 0].set(-2)
    scores = scores.at[0, 0, RB - 1].set(-1)
    order = jnp.argsort(scores, axis=-1, stable=True).astype(jnp.int32)
    return order[:, :, :PER_PEER]


def plant(drawn, stream_key, low, top_value):
    shape = drawn.shape
    spot = [jax.random.randint(jax.random.fold_in(stream_key, axis), (), 0, shape[axis]) for axis in range(len(shape))]
    drawn = drawn.at[tuple(spot)].set(low)
    longest = shape.index(max(shape))
    spot[longest] = (spot[longest] + 1) % shape[longest]
    return drawn.at[tuple(spot)].set(top_value)


def steps_of(stream_key, dims, shards, smallest, top_value):
    loudness = 1.0
    for position, shards_of in shards:
        draws = jax.random.uniform(jax.random.fold_in(jax.random.fold_in(stream_key, 6), position), (shards_of,), jnp.float32, smallest / len(shards), top_value / len(shards))
        loudness = loudness * jnp.repeat(jnp.exp(draws), dims[position] // shards_of).reshape((-1,) + (1,) * (len(dims) - 1 - position))
    return loudness


def normal_values(rng, dims, spread, most, cuts=(), held_as=jnp.bfloat16):
    array = spread * jax.random.normal(rng, dims, jnp.float32)
    if cuts:
        array = array * steps_of(rng, dims, cuts, -0.22, 0.18)
    return jnp.clip(array, -most, most).astype(held_as)


def setup_inputs(seed: int = 0) -> dict:
    seeds = jax.random.split(jax.random.key(seed), 8)
    return {
        "features": normal_values(seeds[0], (NODES, F_IN), 1.0, 6.0, ((0, 16),)),
        "tile_values": normal_values(seeds[1], (N_ROWS, N_REP, TMAX, TILE, TILE), ((TILE * N_REP * TMAX // RB // 3) ** -0.5), 0.1875, ((0, 16), (1, 8))),
        "tile_rows": plant(jax.random.randint(seeds[2], (N_ROWS, N_REP, TMAX), 0, RB), jax.random.fold_in(seeds[2], 1), 0, RB - 1).astype(jnp.int32),
        "tile_slots": plant(jax.random.randint(seeds[3], (N_ROWS, N_REP, TMAX), 0, SLOTS), jax.random.fold_in(seeds[3], 1), 0, SLOTS - 1).astype(jnp.int32),
        "tile_counts": draw_tile_counts(jax.random.fold_in(seeds[7], 71), 0),
        "fetch_lists": draw_fetch_lists(jax.random.fold_in(seeds[7], 71), 0),
        "filter_weights": normal_values(seeds[6], (DEGREE + 1, F_IN, F_OUT), F_IN ** -0.5, 0.5),
    }


def gather_blocks(previous, wanted):
    blocks = previous.reshape(N_ROWS, RB, TILE, F_IN)
    owners = jnp.arange(N_ROWS, dtype=jnp.int32)[:, None]
    return blocks[owners, wanted].reshape(N_ROWS * PER_PEER, TILE, F_IN)


def replica_term(total, fetched, values, rows_of, slots_of, count):
    def one_block(number, running):
        start = number * 64
        part = lax.dynamic_slice_in_dim(values, start, 64, 0).astype(jnp.float32)
        rows_part = lax.dynamic_slice_in_dim(rows_of, start, 64, 0)
        slots_part = lax.dynamic_slice_in_dim(slots_of, start, 64, 0)
        picked = fetched[slots_part].astype(jnp.float32)
        product = jnp.einsum("tij,tjf->tif", part, picked)
        live = (start + jnp.arange(64, dtype=jnp.int32)) < count
        product = jnp.where(live[:, None, None], product, jnp.zeros_like(product))
        return running.at[rows_part].add(product)

    return lax.fori_loop(0, (count + 63) // 64, one_block, total)


def apply_operator(previous, tile_values, tile_rows, tile_slots, tile_counts, fetch_lists):
    def one_owner(inputs):
        values, rows_of, slots_of, counts, wanted = inputs
        fetched = gather_blocks(previous, wanted)
        total = jnp.zeros((RB, TILE, F_IN), jnp.float32)
        for replica in range(N_REP):
            total = replica_term(total, fetched, values[replica], rows_of[replica], slots_of[replica], counts[replica])
        return total

    result = lax.map(one_owner, (tile_values, tile_rows, tile_slots, tile_counts, fetch_lists))
    return result.reshape(NODES, F_IN)


def reference(features, tile_values, tile_rows, tile_slots, tile_counts, fetch_lists, filter_weights):
    terms = [features]
    for degree in range(1, DEGREE + 1):
        total = apply_operator(terms[-1], tile_values, tile_rows, tile_slots, tile_counts, fetch_lists)
        if degree == 1:
            following = total
        else:
            following = 2.0 * total - terms[-2].astype(jnp.float32)
        terms.append(following.astype(jnp.bfloat16))
    output = jnp.zeros((NODES, F_OUT), jnp.float32)
    for degree in range(DEGREE + 1):
        output = output + jnp.dot(terms[degree], filter_weights[degree], preferred_element_type=jnp.float32)
    return output.astype(jnp.bfloat16)
```

```python
import jax
import jax.numpy as jnp
from jax import lax
from jax.experimental import pallas as pl
from jax.experimental.pallas import tpu as pltpu
from jax.sharding import PartitionSpec as P

CHUNK = 32
DEPTH = 4
UNROLL = 32
CORES = 2


def tile_sums(pieces, values, rows_of, slots_of, scalars, row_blocks, whole_blocks):
    arrays = [piece[0] for piece in pieces]
    _, sub, width = arrays[0].shape
    tmax, tile, _ = values.shape
    replicas = tile // sub
    chips = replicas // CORES
    slots = sum(piece[0].shape[0] for piece in pieces) // replicas
    per = row_blocks // replicas

    def body(*refs):
        scalar, rows, slot = refs[:3]
        parts = refs[3 : 3 + len(pieces)]
        vals, peer, mine, fetched, buf, acc, sems, part_sems = refs[3 + len(pieces) :]
        count = scalar[0]
        chip = scalar[1]
        core = scalar[2]
        chunks = (count + CHUNK - 1) // CHUNK

        def copy(number):
            place = lax.rem(number, DEPTH)
            return pltpu.make_async_copy(
                vals.at[pl.ds(number * CHUNK, CHUNK)], buf.at[place], sems.at[place]
            )

        part_copies = []
        for index, (array, hops, other, first) in enumerate(pieces):
            from_core = 1 - core if other else core
            rank = lax.rem(chip + hops + chips, chips) * CORES + from_core
            part_copies.append(
                pltpu.make_async_copy(
                    parts[index],
                    fetched.at[rank, pl.ds(first, array.shape[0])],
                    part_sems.at[index],
                )
            )
        for part_copy in part_copies:
            part_copy.start()
        for number in range(DEPTH - 1):

            @pl.when(number < chunks)
            def _():
                copy(number).start()

        def clear(block, carry):
            acc[block] = jnp.zeros((tile, width), jnp.float32)
            return carry

        lax.fori_loop(0, row_blocks + 1, clear, 0)
        for part_copy in part_copies:
            part_copy.wait()

        def one_chunk(number, carry):
            @pl.when(number + DEPTH - 1 < chunks)
            def _():
                copy(number + DEPTH - 1).start()

            copy(number).wait()
            place = lax.rem(number, DEPTH)

            def group(step, inner):
                products = []
                for unit in range(UNROLL):
                    local = step * UNROLL + unit
                    t = number * CHUNK + local
                    block = fetched[:, slot[t]].reshape(tile, width)
                    target = jnp.where(t < count, rows[t], row_blocks)
                    products.append(
                        (target, jnp.dot(buf[place, local], block, preferred_element_type=jnp.float32))
                    )
                for target, product in products:
                    acc[target] += product
                return inner

            return lax.fori_loop(0, CHUNK // UNROLL, group, carry)

        lax.fori_loop(0, chunks, one_chunk, 0)

        for hops in range(chips):
            for out, from_core in ((peer, 1 - core), (mine, core)):
                rank = lax.rem(chip + hops, chips) * CORES + from_core
                if whole_blocks:
                    share = acc[pl.ds(rank * per, per)].reshape(per * replicas, sub, width)
                else:
                    share = acc[pl.ds(0, row_blocks), pl.ds(pl.multiple_of(rank * sub, sub), sub), :]
                out[hops] = share.astype(out.dtype)

    smem = pl.BlockSpec(memory_space=pltpu.SMEM)
    vmem = pl.BlockSpec(memory_space=pltpu.VMEM)
    hbm = pl.BlockSpec(memory_space=pl.ANY)
    shape = (chips, row_blocks, sub, width)
    return pl.pallas_call(
        body,
        out_shape=(
            jax.ShapeDtypeStruct(shape, jnp.bfloat16),
            jax.ShapeDtypeStruct(shape, jnp.float32),
        ),
        in_specs=[smem, smem, smem] + [hbm] * (len(pieces) + 1),
        out_specs=(vmem, vmem),
        scratch_shapes=[
            pltpu.VMEM((replicas, slots, sub, width), jnp.bfloat16),
            pltpu.VMEM((DEPTH, CHUNK, tile, tile), values.dtype),
            pltpu.VMEM((row_blocks + 1, tile, width), jnp.float32),
            pltpu.SemaphoreType.DMA((DEPTH,)),
            pltpu.SemaphoreType.DMA((len(pieces),)),
        ],
        name="tile_sums",
    )(scalars, rows_of, slots_of, *arrays, values)


def on_device(
    features, tile_values, tile_rows, tile_slots, tile_counts, fetch_lists, filter_weights
):
    values = tile_values[0, 0]
    rows_of = tile_rows[0, 0]
    slots_of = tile_slots[0, 0]
    wanted = fetch_lists[0]
    tile = values.shape[1]
    local_rows, width = features.shape
    row_blocks = local_rows // tile
    replicas = lax.axis_size("rep")
    chips = replicas // CORES
    sub = tile // replicas
    rank = lax.axis_index("rep")
    share_rows = local_rows // replicas
    degree_last = filter_weights.shape[0] - 1
    scalars = jnp.stack([tile_counts[0, 0], rank // CORES, rank % CORES]).astype(jnp.int32)

    def along(x, hops):
        step = CORES * hops
        return lax.ppermute(x, "rep", [((i + step) % replicas, i) for i in range(replicas)])

    def partner(x):
        return lax.ppermute(x, "rep", [(i, i ^ 1) for i in range(replicas)])

    def gather(sent):
        half = sent.shape[0] // 2
        before, after, other = along(sent, -1), along(sent, 1), partner(sent)
        first, second = along(before[:half], -1), along(after[half:], 1)
        pieces = [(sent, 0, False, 0), (other, 0, True, 0)]
        for array, hops, start in (
            (before, -1, 0),
            (after, 1, 0),
            (first, -2, 0),
            (second, 2, half),
        ):
            pieces.append((array, hops, False, start))
            pieces.append((partner(array), hops, True, start))
        return pieces

    def reduce(peer, mine):
        sums = mine + partner(peer).astype(jnp.float32)
        total = sums[0]
        for hops in range(1, chips):
            total = total + along(sums[hops].astype(jnp.bfloat16), -hops).astype(jnp.float32)
        return total

    served = lax.all_to_all(wanted, "rows", split_axis=0, concat_axis=0, tiled=True)
    terms = [
        lax.dynamic_slice_in_dim(
            features.reshape(row_blocks, tile, width), rank * sub, sub, 1
        )
    ]
    own = [lax.dynamic_slice_in_dim(features, rank * share_rows, share_rows, 0)]
    for degree in range(1, degree_last + 1):
        last = degree == degree_last
        if last:
            swapped = jnp.stack(terms[1:], 1).reshape(
                replicas, row_blocks // replicas, degree_last - 1, sub, width
            )
            swapped = lax.all_to_all(swapped, "rep", split_axis=0, concat_axis=0, tiled=True)
            swapped = swapped.transpose(2, 1, 0, 3, 4).reshape(degree_last - 1, share_rows, width)
            own.extend(swapped[k] for k in range(degree_last - 1))
        sent = lax.all_to_all(
            terms[-1][served], "rows", split_axis=0, concat_axis=0, tiled=True
        ).reshape(-1, sub, width)
        peer, mine = tile_sums(
            gather(sent), values, rows_of, slots_of, scalars, row_blocks, whole_blocks=last
        )
        total = reduce(peer, mine)
        if last:
            total = total.reshape(share_rows, width)
            before = own[-2]
        else:
            before = terms[-2] if degree > 1 else None
        following = total if degree == 1 else 2.0 * total - before.astype(jnp.float32)
        (own if last else terms).append(following.astype(jnp.bfloat16))
    output = jnp.zeros((share_rows, filter_weights.shape[2]), jnp.float32)
    for degree in range(degree_last + 1):
        output = output + jnp.dot(
            own[degree], filter_weights[degree], preferred_element_type=jnp.float32
        )
    return output.astype(jnp.bfloat16)


def solution(mesh):
    return jax.shard_map(
        on_device,
        mesh=mesh,
        in_specs=(
            P("rows", None),
            P("rows", "rep", None, None, None),
            P("rows", "rep", None),
            P("rows", "rep", None),
            P("rows", "rep"),
            P("rows", None, None),
            P(),
        ),
        out_specs=P(("rows", "rep"), None),
        check_vma=False,
    )
```

```python
import jax
import jax.numpy as jnp
from jax import lax
from jax.experimental import pallas as pl
from jax.experimental.pallas import tpu as pltpu
from jax.sharding import PartitionSpec as P

UNROLL = 32
CORES = 2


def tile_sums(fetched, values, rows_of, slots_of, scalars, row_blocks, whole_blocks):
    replicas, _, sub, width = fetched.shape
    tile = values.shape[1]
    chips = replicas // CORES
    per = row_blocks // replicas

    def body(scalar, rows, slot, fetched, vals, peer, mine, acc):
        count = scalar[0]
        chip = scalar[1]
        core = scalar[2]

        def clear(block, carry):
            acc[block] = jnp.zeros((tile, width), jnp.float32)
            return carry

        lax.fori_loop(0, row_blocks + 1, clear, 0)

        def group(step, carry):
            products = []
            for unit in range(UNROLL):
                t = step * UNROLL + unit
                block = fetched[:, slot[t]].reshape(tile, width)
                target = jnp.where(t < count, rows[t], row_blocks)
                products.append(
                    (target, jnp.dot(vals[t], block, preferred_element_type=jnp.float32))
                )
            for target, product in products:
                acc[target] += product
            return carry

        lax.fori_loop(0, (count + UNROLL - 1) // UNROLL, group, 0)

        for hops in range(chips):
            for out, from_core in ((peer, 1 - core), (mine, core)):
                rank = lax.rem(chip + hops, chips) * CORES + from_core
                if whole_blocks:
                    share = acc[pl.ds(rank * per, per)].reshape(per * replicas, sub, width)
                else:
                    share = acc[pl.ds(0, row_blocks), pl.ds(pl.multiple_of(rank * sub, sub), sub), :]
                out[hops] = share.astype(out.dtype)

    smem = pl.BlockSpec(memory_space=pltpu.SMEM)
    vmem = pl.BlockSpec(memory_space=pltpu.VMEM)
    shape = (chips, row_blocks, sub, width)
    return pl.pallas_call(
        body,
        out_shape=(
            pltpu.VMEM(shape, jnp.bfloat16),
            pltpu.VMEM(shape, jnp.float32),
        ),
        in_specs=[smem, smem, smem, vmem, vmem],
        out_specs=(vmem, vmem),
        scratch_shapes=[pltpu.VMEM((row_blocks + 1, tile, width), jnp.float32)],
        compiler_params=pltpu.CompilerParams(vmem_limit_bytes=16 * 2**20),
        name="tile_sums",
    )(
        scalars,
        rows_of,
        slots_of,
        pltpu.with_memory_space_constraint(fetched, pltpu.VMEM),
        pltpu.with_memory_space_constraint(values, pltpu.VMEM),
    )


def load_live(values, count, after):
    def body(count, values, after, out, semaphore):
        groups = (count[0, 0] + UNROLL - 1) // UNROLL

        def copy(step):
            part = pl.ds(step * UNROLL, UNROLL)
            return pltpu.make_async_copy(values.at[part], out.at[part], semaphore.at[step])

        def start(step, carry):
            copy(step).start()
            return carry

        def wait(step, carry):
            copy(step).wait()
            return carry

        lax.fori_loop(0, groups, start, 0)
        lax.fori_loop(0, groups, wait, 0)

    return pl.pallas_call(
        body,
        out_shape=pltpu.VMEM(values.shape, values.dtype),
        in_specs=[
            pl.BlockSpec(memory_space=pltpu.SMEM),
            pl.BlockSpec(memory_space=pltpu.HBM),
            pl.BlockSpec(memory_space=pl.ANY),
        ],
        out_specs=pl.BlockSpec(memory_space=pltpu.VMEM),
        scratch_shapes=[pltpu.SemaphoreType.DMA((values.shape[0] // UNROLL,))],
        compiler_params=pltpu.CompilerParams(vmem_limit_bytes=2 * 2**20),
        name="load_live",
    )(count, pltpu.with_memory_space_constraint(values, pltpu.HBM), after)


def on_device(
    features, tile_values, tile_rows, tile_slots, tile_counts, fetch_lists, filter_weights
):
    values = tile_values[0, 0]
    rows_of = tile_rows[0, 0]
    slots_of = tile_slots[0, 0]
    wanted = fetch_lists[0]
    tile = values.shape[1]
    local_rows, width = features.shape
    row_blocks = local_rows // tile
    replicas = lax.axis_size("rep")
    chips = replicas // CORES
    sub = tile // replicas
    rank = lax.axis_index("rep")
    share_rows = local_rows // replicas
    degree_last = filter_weights.shape[0] - 1
    scalars = jnp.stack([tile_counts[0, 0], rank // CORES, rank % CORES]).astype(jnp.int32)

    def along(x, hops):
        step = CORES * hops
        return lax.ppermute(x, "rep", [((i + step) % replicas, i) for i in range(replicas)])

    def partner(x):
        return lax.ppermute(x, "rep", [(i, i ^ 1) for i in range(replicas)])

    def gather(sent):
        chip, core = rank // CORES, rank % CORES
        slots = sent.shape[0]
        half = slots // 2
        before, after, other = along(sent, -1), along(sent, 1), partner(sent)
        live = load_live(values, tile_counts, sent)
        before, live = lax.optimization_barrier((before, live))
        first, second = along(before[:half], -1), along(after[half:], 1)
        fetched = jnp.zeros((replicas, slots, sub, width), sent.dtype)

        def put(fetched, array, hops, from_core, start):
            place = (chip + hops) % chips * CORES + from_core
            return lax.dynamic_update_slice(fetched, array[None], (place, start, 0, 0))

        fetched = put(fetched, sent, 0, core, 0)
        fetched = put(fetched, other, 0, 1 - core, 0)
        for array, hops, start in ((before, -1, 0), (after, 1, 0), (first, 2, 0), (second, 2, half)):
            fetched = put(fetched, array, hops, core, start)
            fetched = put(fetched, partner(array), hops, 1 - core, start)
        return fetched, live

    def reduce(peer, mine):
        sums = mine + partner(peer).astype(jnp.float32)
        sent = [sums[hops].astype(jnp.bfloat16) for hops in range(chips)]
        half = row_blocks // 2
        low, high = along(sent[2][:half], -1), along(sent[2][half:], 1)
        parts = [along(sent[1], -1), along(sent[3], 1)]
        parts.append(jnp.concatenate([along(low, -1), along(high, 1)], 0))
        total = sums[0]
        for part in parts:
            total = total + part.astype(jnp.float32)
        return total

    served = lax.all_to_all(wanted, "rows", split_axis=0, concat_axis=0, tiled=True)
    terms = [
        lax.dynamic_slice_in_dim(
            features.reshape(row_blocks, tile, width), rank * sub, sub, 1
        )
    ]
    own = [lax.dynamic_slice_in_dim(features, rank * share_rows, share_rows, 0)]
    for degree in range(1, degree_last + 1):
        last = degree == degree_last
        if last:
            swapped = jnp.stack(terms[1:], 1).reshape(
                replicas, row_blocks // replicas, degree_last - 1, sub, width
            )
            swapped = lax.all_to_all(swapped, "rep", split_axis=0, concat_axis=0, tiled=True)
            swapped = swapped.transpose(2, 1, 0, 3, 4).reshape(degree_last - 1, share_rows, width)
            own.extend(swapped[k] for k in range(degree_last - 1))
        sent = lax.all_to_all(
            terms[-1][served], "rows", split_axis=0, concat_axis=0, tiled=True
        ).reshape(-1, sub, width)
        fetched, live = gather(sent)
        peer, mine = tile_sums(
            fetched, live, rows_of, slots_of, scalars, row_blocks, whole_blocks=last
        )
        total = reduce(peer, mine)
        if last:
            total = total.reshape(share_rows, width)
            before = own[-2]
        else:
            before = terms[-2] if degree > 1 else None
        following = total if degree == 1 else 2.0 * total - before.astype(jnp.float32)
        (own if last else terms).append(following.astype(jnp.bfloat16))
    output = jnp.zeros((share_rows, filter_weights.shape[2]), jnp.float32)
    for degree in range(degree_last + 1):
        output = output + jnp.dot(
            own[degree], filter_weights[degree], preferred_element_type=jnp.float32
        )
    return output.astype(jnp.bfloat16)


def solution(mesh):
    return jax.shard_map(
        on_device,
        mesh=mesh,
        in_specs=(
            P("rows", None),
            P("rows", "rep", None, None, None),
            P("rows", "rep", None),
            P("rows", "rep", None),
            P("rows", "rep"),
            P("rows", None, None),
            P(),
        ),
        out_specs=P(("rows", "rep"), None),
        check_vma=False,
    )
```

```python
import jax
import jax.numpy as jnp
from jax import lax
from jax.experimental import pallas as pl
from jax.experimental.pallas import tpu as pltpu
from jax.sharding import PartitionSpec as P


UNROLL = 32
CORES = 2


def tile_sums(fetched, values, rows_of, slots_of, scalars, row_blocks, whole_blocks):
    replicas, _, sub, width = fetched.shape
    tile = values.shape[1]
    chips = replicas // CORES
    per = row_blocks // replicas

    def body(scalar, rows, slot, fetched, vals, peer, mine, acc):
        count = scalar[0]
        chip = scalar[1]
        core = scalar[2]

        def clear(block, carry):
            acc[block] = jnp.zeros((tile, width), jnp.float32)
            return carry

        lax.fori_loop(0, row_blocks + 1, clear, 0)

        def group(step, carry):
            products = []
            for unit in range(UNROLL):
                t = step * UNROLL + unit
                block = fetched[:, slot[t]].reshape(tile, width)
                target = jnp.where(t < count, rows[t], row_blocks)
                products.append(
                    (target, jnp.dot(vals[t], block, preferred_element_type=jnp.float32))
                )
            for target, product in products:
                acc[target] += product
            return carry

        lax.fori_loop(0, (count + UNROLL - 1) // UNROLL, group, 0)

        for hops in range(chips):
            for out, from_core in ((peer, 1 - core), (mine, core)):
                rank = lax.rem(chip + hops, chips) * CORES + from_core
                if whole_blocks:
                    share = acc[pl.ds(rank * per, per)].reshape(per * replicas, sub, width)
                else:
                    share = acc[pl.ds(0, row_blocks), pl.ds(pl.multiple_of(rank * sub, sub), sub), :]
                out[hops] = share.astype(out.dtype)

    smem = pl.BlockSpec(memory_space=pltpu.SMEM)
    vmem = pl.BlockSpec(memory_space=pltpu.VMEM)
    shape = (chips, row_blocks, sub, width)
    return pl.pallas_call(
        body,
        out_shape=(
            pltpu.VMEM(shape, jnp.bfloat16),
            pltpu.VMEM(shape, jnp.float32),
        ),
        in_specs=[smem, smem, smem, vmem, vmem],
        out_specs=(vmem, vmem),
        scratch_shapes=[pltpu.VMEM((row_blocks + 1, tile, width), jnp.float32)],
        compiler_params=pltpu.CompilerParams(vmem_limit_bytes=16 * 2**20),
        name="tile_sums",
    )(
        scalars,
        rows_of,
        slots_of,
        pltpu.with_memory_space_constraint(fetched, pltpu.VMEM),
        pltpu.with_memory_space_constraint(values, pltpu.VMEM),
    )


def load_live(values, scalars, after):
    def body(scalar, values, after, out, semaphore):
        groups = (scalar[0] + UNROLL - 1) // UNROLL

        def copy(step):
            part = pl.ds(step * UNROLL, UNROLL)
            return pltpu.make_async_copy(values.at[part], out.at[part], semaphore.at[step])

        def start(step, carry):
            copy(step).start()
            return carry

        def wait(step, carry):
            copy(step).wait()
            return carry

        lax.fori_loop(0, groups, start, 0)
        lax.fori_loop(0, groups, wait, 0)

    return pl.pallas_call(
        body,
        out_shape=pltpu.VMEM(values.shape, values.dtype),
        in_specs=[
            pl.BlockSpec(memory_space=pltpu.SMEM),
            pl.BlockSpec(memory_space=pltpu.HBM),
            pl.BlockSpec(memory_space=pl.ANY),
        ],
        out_specs=pl.BlockSpec(memory_space=pltpu.VMEM),
        scratch_shapes=[pltpu.SemaphoreType.DMA((values.shape[0] // UNROLL,))],
        compiler_params=pltpu.CompilerParams(vmem_limit_bytes=2 * 2**20),
        name="load_live",
    )(scalars, pltpu.with_memory_space_constraint(values, pltpu.HBM), after)


def on_device(
    features, tile_values, tile_rows, tile_slots, tile_counts, fetch_lists, filter_weights
):
    values = tile_values[0, 0]
    rows_of = tile_rows[0, 0]
    slots_of = tile_slots[0, 0]
    wanted = fetch_lists[0]
    tile = values.shape[1]
    local_rows, width = features.shape
    row_blocks = local_rows // tile
    replicas = lax.axis_size("rep")
    chips = replicas // CORES
    sub = tile // replicas
    rank = lax.axis_index("rep")
    share_rows = local_rows // replicas
    degree_last = filter_weights.shape[0] - 1
    chip, core = rank // CORES, rank % CORES
    places = [
        ((chip + hops) % chips * CORES + core, (chip + hops) % chips * CORES + 1 - core)
        for hops in range(chips)
    ]
    scalars = jnp.stack([tile_counts[0, 0], chip, core, *sum(places, ())]).astype(jnp.int32)

    def along(x, hops):
        step = CORES * hops
        return lax.ppermute(x, "rep", [((i + step) % replicas, i) for i in range(replicas)])

    def partner(x):
        return lax.ppermute(x, "rep", [(i, i ^ 1) for i in range(replicas)])

    def gather(sent):
        slots = sent.shape[0]
        half = slots // 2
        low, high = sent[:half], sent[half:]
        before_low, after_high = along(low, -1), along(high, 1)
        before_high, after_low = along(high, -1), along(low, 1)
        other = partner(sent)
        live = load_live(values, scalars, sent)
        before_low, live = lax.optimization_barrier((before_low, live))
        far_low, far_high = along(before_low, -1), along(after_high, 1)
        fetched = jnp.zeros((replicas, slots, sub, width), sent.dtype)

        def put(fetched, array, hops, other_core, start):
            place = places[hops][other_core]
            return lax.dynamic_update_slice(
                fetched, array[None], (place, start, 0, 0), allow_negative_indices=False
            )

        fetched = put(fetched, sent, 0, 0, 0)
        fetched = put(fetched, other, 0, 1, 0)
        for array, hops, start in (
            (before_low, -1, 0),
            (after_high, 1, half),
            (before_high, -1, half),
            (after_low, 1, 0),
            (far_low, 2, 0),
            (far_high, 2, half),
        ):
            fetched = put(fetched, array, hops, 0, start)
            crossed = partner(array)
            fetched = put(fetched, crossed, hops, 1, start)
        return fetched, live

    def reduce(peer, mine):
        sums = mine + partner(peer).astype(jnp.float32)
        sent = [sums[hops].astype(jnp.bfloat16) for hops in range(chips)]
        half = row_blocks // 2
        low, high = along(sent[2][:half], -1), along(sent[2][half:], 1)
        parts = [along(sent[1], -1), along(sent[3], 1)]
        parts.append(jnp.concatenate([along(low, -1), along(high, 1)], 0))
        total = sums[0]
        for part in parts:
            total = total + part.astype(jnp.float32)
        return total

    served = lax.all_to_all(wanted, "rows", split_axis=0, concat_axis=0, tiled=True)
    terms = [
        lax.dynamic_slice_in_dim(
            features.reshape(row_blocks, tile, width), rank * sub, sub, 1
        )
    ]
    own = [lax.dynamic_slice_in_dim(features, rank * share_rows, share_rows, 0)]

    def step(degree):
        last = degree == degree_last
        if last:
            swapped = jnp.stack(terms[1:], 1).reshape(
                replicas, row_blocks // replicas, degree_last - 1, sub, width
            )
            swapped = lax.all_to_all(swapped, "rep", split_axis=0, concat_axis=0, tiled=True)
            swapped = swapped.transpose(2, 1, 0, 3, 4).reshape(degree_last - 1, share_rows, width)
            own.extend(swapped[k] for k in range(degree_last - 1))
        sent = lax.all_to_all(
            terms[-1][served], "rows", split_axis=0, concat_axis=0, tiled=True
        ).reshape(-1, sub, width)
        fetched, live = gather(sent)
        peer, mine = tile_sums(
            fetched, live, rows_of, slots_of, scalars, row_blocks, whole_blocks=last
        )
        total = reduce(peer, mine)
        if last:
            total = total.reshape(share_rows, width)
            before = own[-2]
        else:
            before = terms[-2] if degree > 1 else None
        following = total if degree == 1 else 2.0 * total - before.astype(jnp.float32)
        (own if last else terms).append(following.astype(jnp.bfloat16))

    for degree in range(1, degree_last + 1):
        step(degree)
    output = jnp.zeros((share_rows, filter_weights.shape[2]), jnp.float32)
    for degree in range(degree_last + 1):
        output = output + jnp.dot(
            own[degree], filter_weights[degree], preferred_element_type=jnp.float32
        )
    return output.astype(jnp.bfloat16)


def solution(mesh):
    return jax.shard_map(
        on_device,
        mesh=mesh,
        in_specs=(
            P("rows", None),
            P("rows", "rep", None, None, None),
            P("rows", "rep", None),
            P("rows", "rep", None),
            P("rows", "rep"),
            P("rows", None, None),
            P(),
        ),
        out_specs=P(("rows", "rep"), None),
        check_vma=False,
    )
```

```python
import jax
import jax.numpy as jnp
from jax import lax
from jax.experimental import pallas as pl
from jax.experimental.pallas import tpu as pltpu
from jax.sharding import PartitionSpec as P


UNROLL = 32
CORES = 2


def tile_sums(fetched, values, rows_of, slots_of, scalars, row_blocks, whole_blocks):
    replicas, _, sub, width = fetched.shape
    tile = values.shape[1]
    chips = replicas // CORES
    per = row_blocks // replicas

    def body(scalar, rows, slot, fetched, vals, peer, mine, acc):
        count = scalar[0]
        chip = scalar[1]
        core = scalar[2]

        def clear(block, carry):
            acc[block] = jnp.zeros((tile, width), jnp.float32)
            return carry

        lax.fori_loop(0, row_blocks + 1, clear, 0)

        def group(step, carry):
            products = []
            for unit in range(UNROLL):
                t = step * UNROLL + unit
                block = fetched[:, slot[t]].reshape(tile, width)
                target = jnp.where(t < count, rows[t], row_blocks)
                products.append(
                    (target, jnp.dot(vals[t], block, preferred_element_type=jnp.float32))
                )
            for target, product in products:
                acc[target] += product
            return carry

        lax.fori_loop(0, (count + UNROLL - 1) // UNROLL, group, 0)

        for hops in range(chips):
            for out, from_core in ((peer, 1 - core), (mine, core)):
                rank = lax.rem(chip + hops, chips) * CORES + from_core
                if whole_blocks:
                    share = acc[pl.ds(rank * per, per)].reshape(per * replicas, sub, width)
                else:
                    share = acc[pl.ds(0, row_blocks), pl.ds(pl.multiple_of(rank * sub, sub), sub), :]
                out[hops] = share.astype(out.dtype)

    smem = pl.BlockSpec(memory_space=pltpu.SMEM)
    vmem = pl.BlockSpec(memory_space=pltpu.VMEM)
    shape = (chips, row_blocks, sub, width)
    return pl.pallas_call(
        body,
        out_shape=(
            pltpu.VMEM(shape, jnp.bfloat16),
            pltpu.VMEM(shape, jnp.float32),
        ),
        in_specs=[smem, smem, smem, vmem, vmem],
        out_specs=(vmem, vmem),
        scratch_shapes=[pltpu.VMEM((row_blocks + 1, tile, width), jnp.float32)],
        compiler_params=pltpu.CompilerParams(vmem_limit_bytes=16 * 2**20),
        name="tile_sums",
    )(
        scalars,
        rows_of,
        slots_of,
        pltpu.with_memory_space_constraint(fetched, pltpu.VMEM),
        pltpu.with_memory_space_constraint(values, pltpu.VMEM),
    )


def load_live(values, scalars, after):
    def body(scalar, values, after, out, semaphore):
        groups = (scalar[0] + UNROLL - 1) // UNROLL

        def copy(step):
            part = pl.ds(step * UNROLL, UNROLL)
            return pltpu.make_async_copy(values.at[part], out.at[part], semaphore.at[step])

        def start(step, carry):
            copy(step).start()
            return carry

        def wait(step, carry):
            copy(step).wait()
            return carry

        lax.fori_loop(0, groups, start, 0)
        lax.fori_loop(0, groups, wait, 0)

    return pl.pallas_call(
        body,
        out_shape=pltpu.VMEM(values.shape, values.dtype),
        in_specs=[
            pl.BlockSpec(memory_space=pltpu.SMEM),
            pl.BlockSpec(memory_space=pltpu.HBM),
            pl.BlockSpec(memory_space=pl.ANY),
        ],
        out_specs=pl.BlockSpec(memory_space=pltpu.VMEM),
        scratch_shapes=[pltpu.SemaphoreType.DMA((values.shape[0] // UNROLL,))],
        compiler_params=pltpu.CompilerParams(vmem_limit_bytes=2 * 2**20),
        name="load_live",
    )(scalars, pltpu.with_memory_space_constraint(values, pltpu.HBM), after)


def on_device(
    features, tile_values, tile_rows, tile_slots, tile_counts, fetch_lists, filter_weights
):
    values = tile_values[0, 0]
    rows_of = tile_rows[0, 0]
    slots_of = tile_slots[0, 0]
    wanted = fetch_lists[0]
    tile = values.shape[1]
    local_rows, width = features.shape
    row_blocks = local_rows // tile
    replicas = lax.axis_size("rep")
    chips = replicas // CORES
    sub = tile // replicas
    rank = lax.axis_index("rep")
    share_rows = local_rows // replicas
    degree_last = filter_weights.shape[0] - 1
    chip, core = rank // CORES, rank % CORES
    places = [
        ((chip + hops) % chips * CORES + core, (chip + hops) % chips * CORES + 1 - core)
        for hops in range(chips)
    ]
    scalars = jnp.stack([tile_counts[0, 0], chip, core, *sum(places, ())]).astype(jnp.int32)

    def along(x, hops):
        step = CORES * hops
        return lax.ppermute(x, "rep", [((i + step) % replicas, i) for i in range(replicas)])

    def partner(x):
        return lax.ppermute(x, "rep", [(i, i ^ 1) for i in range(replicas)])

    def gather(sent):
        slots = sent.shape[0]
        half = slots // 2
        before, after, other = along(sent, -1), along(sent, 1), partner(sent)
        first, second = along(before[:half], -1), along(after[half:], 1)
        live = load_live(values, scalars, sent)
        fetched = jnp.zeros((replicas, slots, sub, width), sent.dtype)

        def put(fetched, array, hops, other_core, start):
            place = places[hops][other_core]
            return lax.dynamic_update_slice(
                fetched, array[None], (place, start, 0, 0), allow_negative_indices=False
            )

        fetched = put(fetched, sent, 0, 0, 0)
        fetched = put(fetched, other, 0, 1, 0)
        for array, hops, start in ((before, -1, 0), (after, 1, 0), (first, 2, 0), (second, 2, half)):
            fetched = put(fetched, array, hops, 0, start)
            fetched = put(fetched, partner(array), hops, 1, start)
        return fetched, live

    def reduce(peer, mine, degree):
        sums = mine + partner(peer).astype(jnp.float32)
        sent = sums.astype(jnp.bfloat16)
        if degree == 1:
            order = (jnp.arange(chips) - chip) % chips
            groups = [list(range(c, replicas, CORES)) for c in range(CORES)]
            moved = lax.all_to_all(
                sent[order], "rep", split_axis=0, concat_axis=0, axis_index_groups=groups, tiled=True
            )
            total = sums[0]
            for place in range(chips):
                part = moved[place].astype(jnp.float32)
                total = total + jnp.where(place == chip, jnp.zeros_like(part), part)
            return total
        if degree == 2:
            parts = [along(sent[hops], -hops) for hops in range(1, chips)]
        else:
            half = row_blocks // 2
            low = along(jnp.concatenate([sent[1], sent[2][:half]], 0), -1)
            high = along(jnp.concatenate([sent[3], sent[2][half:]], 0), 1)
            parts = [low[:row_blocks], high[:row_blocks]]
            parts.append(
                jnp.concatenate([along(low[row_blocks:], -1), along(high[row_blocks:], 1)], 0)
            )
        total = sums[0]
        for part in parts:
            total = total + part.astype(jnp.float32)
        return total

    served = lax.all_to_all(wanted, "rows", split_axis=0, concat_axis=0, tiled=True)
    terms = [
        lax.dynamic_slice_in_dim(
            features.reshape(row_blocks, tile, width), rank * sub, sub, 1
        )
    ]
    own = [lax.dynamic_slice_in_dim(features, rank * share_rows, share_rows, 0)]

    def step(degree):
        last = degree == degree_last
        if last:
            swapped = jnp.stack(terms[1:], 1).reshape(
                replicas, row_blocks // replicas, degree_last - 1, sub, width
            )
            swapped = lax.all_to_all(swapped, "rep", split_axis=0, concat_axis=0, tiled=True)
            swapped = swapped.transpose(2, 1, 0, 3, 4).reshape(degree_last - 1, share_rows, width)
            own.extend(swapped[k] for k in range(degree_last - 1))
        sent = lax.all_to_all(
            terms[-1][served], "rows", split_axis=0, concat_axis=0, tiled=True
        ).reshape(-1, sub, width)
        fetched, live = gather(sent)
        peer, mine = tile_sums(
            fetched, live, rows_of, slots_of, scalars, row_blocks, whole_blocks=last
        )
        total = reduce(peer, mine, degree)
        if last:
            total = total.reshape(share_rows, width)
            before = own[-2]
        else:
            before = terms[-2] if degree > 1 else None
        following = total if degree == 1 else 2.0 * total - before.astype(jnp.float32)
        (own if last else terms).append(following.astype(jnp.bfloat16))

    for degree in range(1, degree_last + 1):
        step(degree)
    output = jnp.zeros((share_rows, filter_weights.shape[2]), jnp.float32)
    for degree in range(degree_last + 1):
        output = output + jnp.dot(
            own[degree], filter_weights[degree], preferred_element_type=jnp.float32
        )
    return output.astype(jnp.bfloat16)


def solution(mesh):
    return jax.shard_map(
        on_device,
        mesh=mesh,
        in_specs=(
            P("rows", None),
            P("rows", "rep", None, None, None),
            P("rows", "rep", None),
            P("rows", "rep", None),
            P("rows", "rep"),
            P("rows", None, None),
            P(),
        ),
        out_specs=P(("rows", "rep"), None),
        check_vma=False,
    )
```

```python
import jax
import jax.numpy as jnp
from jax import lax
from jax.experimental import pallas as pl
from jax.experimental.pallas import tpu as pltpu
from jax.sharding import PartitionSpec as P


UNROLL = 32
CORES = 2


def tile_sums(fetched, values, rows_of, slots_of, scalars, row_blocks, whole_blocks):
    replicas, _, sub, width = fetched.shape
    tile = values.shape[1]
    chips = replicas // CORES
    per = row_blocks // replicas

    def body(scalar, rows, slot, fetched, vals, peer, mine, acc):
        count = scalar[0]
        chip = scalar[1]
        core = scalar[2]

        def clear(block, carry):
            acc[block] = jnp.zeros((tile, width), jnp.float32)
            return carry

        lax.fori_loop(0, row_blocks + 1, clear, 0)

        def group(step, carry):
            products = []
            for unit in range(UNROLL):
                t = step * UNROLL + unit
                block = fetched[:, slot[t]].reshape(tile, width)
                target = jnp.where(t < count, rows[t], row_blocks)
                products.append(
                    (target, jnp.dot(vals[t], block, preferred_element_type=jnp.float32))
                )
            for target, product in products:
                acc[target] += product
            return carry

        lax.fori_loop(0, (count + UNROLL - 1) // UNROLL, group, 0)

        for hops in range(chips):
            for out, from_core in ((peer, 1 - core), (mine, core)):
                rank = lax.rem(chip + hops, chips) * CORES + from_core
                if whole_blocks:
                    share = acc[pl.ds(rank * per, per)].reshape(per * replicas, sub, width)
                else:
                    share = acc[pl.ds(0, row_blocks), pl.ds(pl.multiple_of(rank * sub, sub), sub), :]
                out[hops] = share.astype(out.dtype)

    smem = pl.BlockSpec(memory_space=pltpu.SMEM)
    vmem = pl.BlockSpec(memory_space=pltpu.VMEM)
    shape = (chips, row_blocks, sub, width)
    return pl.pallas_call(
        body,
        out_shape=(
            pltpu.VMEM(shape, jnp.bfloat16),
            pltpu.VMEM(shape, jnp.float32),
        ),
        in_specs=[smem, smem, smem, vmem, vmem],
        out_specs=(vmem, vmem),
        scratch_shapes=[pltpu.VMEM((row_blocks + 1, tile, width), jnp.float32)],
        compiler_params=pltpu.CompilerParams(vmem_limit_bytes=16 * 2**20),
        name="tile_sums",
    )(
        scalars,
        rows_of,
        slots_of,
        pltpu.with_memory_space_constraint(fetched, pltpu.VMEM),
        pltpu.with_memory_space_constraint(values, pltpu.VMEM),
    )


def load_live(values, scalars, after):
    def body(scalar, values, after, out, semaphore):
        groups = (scalar[0] + UNROLL - 1) // UNROLL

        def copy(step):
            part = pl.ds(step * UNROLL, UNROLL)
            return pltpu.make_async_copy(values.at[part], out.at[part], semaphore.at[step])

        def start(step, carry):
            copy(step).start()
            return carry

        def wait(step, carry):
            copy(step).wait()
            return carry

        lax.fori_loop(0, groups, start, 0)
        lax.fori_loop(0, groups, wait, 0)

    return pl.pallas_call(
        body,
        out_shape=pltpu.VMEM(values.shape, values.dtype),
        in_specs=[
            pl.BlockSpec(memory_space=pltpu.SMEM),
            pl.BlockSpec(memory_space=pltpu.HBM),
            pl.BlockSpec(memory_space=pl.ANY),
        ],
        out_specs=pl.BlockSpec(memory_space=pltpu.VMEM),
        scratch_shapes=[pltpu.SemaphoreType.DMA((values.shape[0] // UNROLL,))],
        compiler_params=pltpu.CompilerParams(vmem_limit_bytes=2 * 2**20),
        name="load_live",
    )(scalars, pltpu.with_memory_space_constraint(values, pltpu.HBM), after)


def on_device(
    features, tile_values, tile_rows, tile_slots, tile_counts, fetch_lists, filter_weights
):
    values = tile_values[0, 0]
    rows_of = tile_rows[0, 0]
    slots_of = tile_slots[0, 0]
    wanted = fetch_lists[0]
    tile = values.shape[1]
    local_rows, width = features.shape
    row_blocks = local_rows // tile
    replicas = lax.axis_size("rep")
    chips = replicas // CORES
    sub = tile // replicas
    rank = lax.axis_index("rep")
    share_rows = local_rows // replicas
    degree_last = filter_weights.shape[0] - 1
    chip, core = rank // CORES, rank % CORES
    places = [
        ((chip + hops) % chips * CORES + core, (chip + hops) % chips * CORES + 1 - core)
        for hops in range(chips)
    ]
    scalars = jnp.stack([tile_counts[0, 0], chip, core, *sum(places, ())]).astype(jnp.int32)

    def along(x, hops):
        step = CORES * hops
        return lax.ppermute(x, "rep", [((i + step) % replicas, i) for i in range(replicas)])

    def partner(x):
        return lax.ppermute(x, "rep", [(i, i ^ 1) for i in range(replicas)])

    def gather(sent, opposite=None):
        slots = sent.shape[0]
        half = slots // 2
        before, after, other = along(sent, -1), along(sent, 1), partner(sent)
        live = load_live(values, scalars, sent)
        pieces = [(before, -1, 0), (after, 1, 0)]
        if opposite is None:
            first, second = along(before[:half], -1), along(after[half:], 1)
            pieces += [(first, 2, 0), (second, 2, half)]
        else:
            pieces = [(opposite, 2, 0)] + pieces

        def put(fetched, array, hops, other_core, start):
            place = places[hops][other_core]
            return lax.dynamic_update_slice(
                fetched, array[None], (place, start, 0, 0), allow_negative_indices=False
            )

        fetched = jnp.zeros((replicas, slots, sub, width), sent.dtype)
        fetched = put(fetched, sent, 0, 0, 0)
        fetched = put(fetched, other, 0, 1, 0)
        for array, hops, start in pieces:
            fetched = put(fetched, array, hops, 0, start)
            fetched = put(fetched, partner(array), hops, 1, start)
        return fetched, live

    def reduce(peer, mine):
        sums = mine + partner(peer).astype(jnp.float32)
        total = sums[0]
        for hops in range(1, chips):
            total = total + along(sums[hops].astype(jnp.bfloat16), -hops).astype(jnp.float32)
        return total

    served = lax.all_to_all(wanted, "rows", split_axis=0, concat_axis=0, tiled=True)
    blocks = features.reshape(row_blocks, tile, width)
    terms = [lax.dynamic_slice_in_dim(blocks, rank * sub, sub, 1)]
    opposite = lax.dynamic_slice_in_dim(blocks, places[2][0] * sub, sub, 1)
    own = [lax.dynamic_slice_in_dim(features, rank * share_rows, share_rows, 0)]

    def step(degree):
        last = degree == degree_last
        if last:
            swapped = jnp.stack(terms[1:], 1).reshape(
                replicas, row_blocks // replicas, degree_last - 1, sub, width
            )
            swapped = lax.all_to_all(swapped, "rep", split_axis=0, concat_axis=0, tiled=True)
            swapped = swapped.transpose(2, 1, 0, 3, 4).reshape(degree_last - 1, share_rows, width)
            own.extend(swapped[k] for k in range(degree_last - 1))
        if degree == 1:
            both = jnp.concatenate([terms[0], opposite], 1)[served]
            both = lax.all_to_all(both, "rows", split_axis=0, concat_axis=0, tiled=True)
            both = both.reshape(-1, 2 * sub, width)
            fetched, live = gather(both[:, :sub], both[:, sub:])
        else:
            sent = lax.all_to_all(
                terms[-1][served], "rows", split_axis=0, concat_axis=0, tiled=True
            ).reshape(-1, sub, width)
            fetched, live = gather(sent)
        peer, mine = tile_sums(
            fetched, live, rows_of, slots_of, scalars, row_blocks, whole_blocks=last
        )
        total = reduce(peer, mine)
        if last:
            total = total.reshape(share_rows, width)
            before = own[-2]
        else:
            before = terms[-2] if degree > 1 else None
        following = total if degree == 1 else 2.0 * total - before.astype(jnp.float32)
        (own if last else terms).append(following.astype(jnp.bfloat16))

    for degree in range(1, degree_last + 1):
        step(degree)
    output = jnp.zeros((share_rows, filter_weights.shape[2]), jnp.float32)
    for degree in range(degree_last + 1):
        output = output + jnp.dot(
            own[degree], filter_weights[degree], preferred_element_type=jnp.float32
        )
    return output.astype(jnp.bfloat16)


def solution(mesh):
    return jax.shard_map(
        on_device,
        mesh=mesh,
        in_specs=(
            P("rows", None),
            P("rows", "rep", None, None, None),
            P("rows", "rep", None),
            P("rows", "rep", None),
            P("rows", "rep"),
            P("rows", None, None),
            P(),
        ),
        out_specs=P(("rows", "rep"), None),
        check_vma=False,
    )
```

```python
import jax
import jax.numpy as jnp
from jax import lax
from jax.experimental import pallas as pl
from jax.experimental.pallas import tpu as pltpu
from jax.sharding import PartitionSpec as P


UNROLL = 32
CORES = 2


def tile_sums(fetched, values, rows_of, slots_of, scalars, row_blocks, whole_blocks):
    replicas, _, sub, width = fetched.shape
    tile = values.shape[1]
    chips = replicas // CORES
    per = row_blocks // replicas

    def body(scalar, rows, slot, fetched, vals, peer, mine, acc):
        count = scalar[0]
        chip = scalar[1]
        core = scalar[2]

        def clear(block, carry):
            acc[block] = jnp.zeros((tile, width), jnp.float32)
            return carry

        lax.fori_loop(0, row_blocks + 1, clear, 0)

        def group(step, carry):
            products = []
            for unit in range(UNROLL):
                t = step * UNROLL + unit
                block = fetched[:, slot[t]].reshape(tile, width)
                target = jnp.where(t < count, rows[t], row_blocks)
                products.append(
                    (target, jnp.dot(vals[t], block, preferred_element_type=jnp.float32))
                )
            for target, product in products:
                acc[target] += product
            return carry

        lax.fori_loop(0, (count + UNROLL - 1) // UNROLL, group, 0)

        for hops in range(chips):
            for out, from_core in ((peer, 1 - core), (mine, core)):
                rank = lax.rem(chip + hops, chips) * CORES + from_core
                if whole_blocks:
                    share = acc[pl.ds(rank * per, per)].reshape(per * replicas, sub, width)
                else:
                    share = acc[pl.ds(0, row_blocks), pl.ds(pl.multiple_of(rank * sub, sub), sub), :]
                out[hops] = share.astype(out.dtype)

    smem = pl.BlockSpec(memory_space=pltpu.SMEM)
    vmem = pl.BlockSpec(memory_space=pltpu.VMEM)
    shape = (chips, row_blocks, sub, width)
    return pl.pallas_call(
        body,
        out_shape=(
            pltpu.VMEM(shape, jnp.bfloat16),
            pltpu.VMEM(shape, jnp.float32),
        ),
        in_specs=[smem, smem, smem, vmem, vmem],
        out_specs=(vmem, vmem),
        scratch_shapes=[pltpu.VMEM((row_blocks + 1, tile, width), jnp.float32)],
        compiler_params=pltpu.CompilerParams(vmem_limit_bytes=16 * 2**20),
        name="tile_sums",
    )(
        scalars,
        rows_of,
        slots_of,
        pltpu.with_memory_space_constraint(fetched, pltpu.VMEM),
        pltpu.with_memory_space_constraint(values, pltpu.VMEM),
    )


def load_live(values, scalars, sent, replicas):
    def body(scalar, values, sent, live, fetched, semaphore):
        groups = (scalar[0] + UNROLL - 1) // UNROLL

        def copy(step):
            part = pl.ds(step * UNROLL, UNROLL)
            return pltpu.make_async_copy(values.at[part], live.at[part], semaphore.at[step])

        def start(step, carry):
            copy(step).start()
            return carry

        def wait(step, carry):
            copy(step).wait()
            return carry

        lax.fori_loop(0, groups, start, 0)
        fetched[pl.ds(scalar[3], 1)] = sent[...][None]
        lax.fori_loop(0, groups, wait, 0)

    return pl.pallas_call(
        body,
        out_shape=(
            pltpu.VMEM(values.shape, values.dtype),
            pltpu.VMEM((replicas, *sent.shape), sent.dtype),
        ),
        in_specs=[
            pl.BlockSpec(memory_space=pltpu.SMEM),
            pl.BlockSpec(memory_space=pltpu.HBM),
            pl.BlockSpec(memory_space=pltpu.VMEM),
        ],
        out_specs=(
            pl.BlockSpec(memory_space=pltpu.VMEM),
            pl.BlockSpec(memory_space=pltpu.VMEM),
        ),
        scratch_shapes=[pltpu.SemaphoreType.DMA((values.shape[0] // UNROLL,))],
        compiler_params=pltpu.CompilerParams(vmem_limit_bytes=2 * 2**20),
        name="load_live",
    )(
        scalars,
        pltpu.with_memory_space_constraint(values, pltpu.HBM),
        pltpu.with_memory_space_constraint(sent, pltpu.VMEM),
    )


def on_device(
    features, tile_values, tile_rows, tile_slots, tile_counts, fetch_lists, filter_weights
):
    values = tile_values[0, 0]
    rows_of = tile_rows[0, 0]
    slots_of = tile_slots[0, 0]
    wanted = fetch_lists[0]
    tile = values.shape[1]
    local_rows, width = features.shape
    row_blocks = local_rows // tile
    replicas = lax.axis_size("rep")
    chips = replicas // CORES
    sub = tile // replicas
    rank = lax.axis_index("rep")
    share_rows = local_rows // replicas
    degree_last = filter_weights.shape[0] - 1
    chip, core = rank // CORES, rank % CORES
    places = [
        ((chip + hops) % chips * CORES + core, (chip + hops) % chips * CORES + 1 - core)
        for hops in range(chips)
    ]
    scalars = jnp.stack([tile_counts[0, 0], chip, core, *sum(places, ())]).astype(jnp.int32)

    def along(x, hops):
        step = CORES * hops
        return lax.ppermute(x, "rep", [((i + step) % replicas, i) for i in range(replicas)])

    def partner(x):
        return lax.ppermute(x, "rep", [(i, i ^ 1) for i in range(replicas)])

    def gather(sent):
        half = sent.shape[0] // 2
        before, after, other = along(sent, -1), along(sent, 1), partner(sent)
        live, fetched = load_live(values, scalars, sent, replicas)
        first, second = along(before[:half], -1), along(after[half:], 1)
        crossed = [partner(before), partner(after)]
        crossed += [partner(first), partner(second)]

        def put(fetched, array, hops, other_core, start):
            place = places[hops][other_core]
            return lax.dynamic_update_slice(
                fetched, array[None], (place, start, 0, 0), allow_negative_indices=False
            )

        fetched = put(fetched, other, 0, 1, 0)
        for array, across, hops, start in zip(
            (before, after, first, second), crossed, (-1, 1, 2, 2), (0, 0, 0, half)
        ):
            fetched = put(fetched, array, hops, 0, start)
            fetched = put(fetched, across, hops, 1, start)
        return fetched, live

    def swap(term):
        parts = lax.all_to_all(
            term.reshape(replicas, -1, sub, width), "rep", split_axis=0, concat_axis=0, tiled=True
        )
        return parts.transpose(1, 0, 2, 3).reshape(share_rows, width)

    def reduce(peer, mine):
        sums = mine + partner(peer).astype(jnp.float32)
        sent = [sums[hops].astype(jnp.bfloat16) for hops in range(chips)]
        half = row_blocks // 2
        low, high = along(sent[2][:half], -1), along(sent[2][half:], 1)
        parts = [along(sent[1], -1), along(sent[3], 1)]
        parts.append(jnp.concatenate([along(low, -1), along(high, 1)], 0))
        total = sums[0]
        for part in parts:
            total = total + part.astype(jnp.float32)
        return total

    served = lax.all_to_all(wanted, "rows", split_axis=0, concat_axis=0, tiled=True)
    blocks = features.reshape(row_blocks, tile, width)
    terms = [lax.dynamic_slice_in_dim(blocks, rank * sub, sub, 1)]
    own = [lax.dynamic_slice_in_dim(features, rank * share_rows, share_rows, 0)]

    def step(degree):
        last = degree == degree_last
        if degree > 1:
            own.append(swap(terms[-1]))
        sent = lax.all_to_all(
            terms[-1][served], "rows", split_axis=0, concat_axis=0, tiled=True
        ).reshape(-1, sub, width)
        fetched, live = gather(sent)
        peer, mine = tile_sums(
            fetched, live, rows_of, slots_of, scalars, row_blocks, whole_blocks=last
        )
        total = reduce(peer, mine)
        if last:
            total = total.reshape(share_rows, width)
            before = own[-2]
        else:
            before = terms[-2] if degree > 1 else None
        following = total if degree == 1 else 2.0 * total - before.astype(jnp.float32)
        (own if last else terms).append(following.astype(jnp.bfloat16))

    for degree in range(1, degree_last + 1):
        step(degree)
    output = jnp.zeros((share_rows, filter_weights.shape[2]), jnp.float32)
    for degree in range(degree_last + 1):
        output = output + jnp.dot(
            own[degree], filter_weights[degree], preferred_element_type=jnp.float32
        )
    return output.astype(jnp.bfloat16)


def solution(mesh):
    return jax.shard_map(
        on_device,
        mesh=mesh,
        in_specs=(
            P("rows", None),
            P("rows", "rep", None, None, None),
            P("rows", "rep", None),
            P("rows", "rep", None),
            P("rows", "rep"),
            P("rows", None, None),
            P(),
        ),
        out_specs=P(("rows", "rep"), None),
        check_vma=False,
    )
```

```python
import jax
import jax.numpy as jnp
from jax import lax
from jax.experimental import pallas as pl
from jax.experimental.pallas import tpu as pltpu
from jax.sharding import PartitionSpec as P


UNROLL = 32
CORES = 2


def tile_sums(fetched, values, rows_of, slots_of, scalars, row_blocks, whole_blocks):
    replicas, _, sub, width = fetched.shape
    tile = values.shape[1]
    chips = replicas // CORES
    per = row_blocks // replicas

    def body(scalar, rows, slot, fetched, vals, peer, mine, acc):
        count = scalar[0]
        chip = scalar[1]
        core = scalar[2]

        def clear(block, carry):
            acc[block] = jnp.zeros((tile, width), jnp.float32)
            return carry

        lax.fori_loop(0, row_blocks + 1, clear, 0)

        def group(step, carry):
            products = []
            for unit in range(UNROLL):
                t = step * UNROLL + unit
                block = fetched[:, slot[t]].reshape(tile, width)
                target = jnp.where(t < count, rows[t], row_blocks)
                products.append(
                    (target, jnp.dot(vals[t], block, preferred_element_type=jnp.float32))
                )
            for target, product in products:
                acc[target] += product
            return carry

        lax.fori_loop(0, (count + UNROLL - 1) // UNROLL, group, 0)

        for hops in range(chips):
            for out, from_core in ((peer, 1 - core), (mine, core)):
                rank = lax.rem(chip + hops, chips) * CORES + from_core
                if whole_blocks:
                    share = acc[pl.ds(rank * per, per)].reshape(per * replicas, sub, width)
                else:
                    share = acc[pl.ds(0, row_blocks), pl.ds(pl.multiple_of(rank * sub, sub), sub), :]
                out[hops] = share.astype(out.dtype)

    smem = pl.BlockSpec(memory_space=pltpu.SMEM)
    vmem = pl.BlockSpec(memory_space=pltpu.VMEM)
    shape = (chips, row_blocks, sub, width)
    return pl.pallas_call(
        body,
        out_shape=(
            pltpu.VMEM(shape, jnp.bfloat16),
            pltpu.VMEM(shape, jnp.float32),
        ),
        in_specs=[smem, smem, smem, vmem, vmem],
        out_specs=(vmem, vmem),
        scratch_shapes=[pltpu.VMEM((row_blocks + 1, tile, width), jnp.float32)],
        compiler_params=pltpu.CompilerParams(vmem_limit_bytes=16 * 2**20),
        name="tile_sums",
    )(
        scalars,
        rows_of,
        slots_of,
        pltpu.with_memory_space_constraint(fetched, pltpu.VMEM),
        pltpu.with_memory_space_constraint(values, pltpu.VMEM),
    )


def load_live(values, scalars, sent, replicas):
    def body(scalar, values, sent, live, fetched, semaphore):
        groups = (scalar[0] + UNROLL - 1) // UNROLL

        def copy(step):
            part = pl.ds(step * UNROLL, UNROLL)
            return pltpu.make_async_copy(values.at[part], live.at[part], semaphore.at[step])

        def start(step, carry):
            copy(step).start()
            return carry

        def wait(step, carry):
            copy(step).wait()
            return carry

        lax.fori_loop(0, groups, start, 0)
        fetched[pl.ds(scalar[3], 1)] = sent[...][None]
        lax.fori_loop(0, groups, wait, 0)

    return pl.pallas_call(
        body,
        out_shape=(
            pltpu.VMEM(values.shape, values.dtype),
            pltpu.VMEM((replicas, *sent.shape), sent.dtype),
        ),
        in_specs=[
            pl.BlockSpec(memory_space=pltpu.SMEM),
            pl.BlockSpec(memory_space=pltpu.HBM),
            pl.BlockSpec(memory_space=pltpu.VMEM),
        ],
        out_specs=(
            pl.BlockSpec(memory_space=pltpu.VMEM),
            pl.BlockSpec(memory_space=pltpu.VMEM),
        ),
        scratch_shapes=[pltpu.SemaphoreType.DMA((values.shape[0] // UNROLL,))],
        compiler_params=pltpu.CompilerParams(vmem_limit_bytes=2 * 2**20),
        name="load_live",
    )(
        scalars,
        pltpu.with_memory_space_constraint(values, pltpu.HBM),
        pltpu.with_memory_space_constraint(sent, pltpu.VMEM),
    )


def on_device(
    features, tile_values, tile_rows, tile_slots, tile_counts, fetch_lists, filter_weights
):
    values = tile_values[0, 0]
    rows_of = tile_rows[0, 0]
    slots_of = tile_slots[0, 0]
    wanted = fetch_lists[0]
    tile = values.shape[1]
    local_rows, width = features.shape
    row_blocks = local_rows // tile
    replicas = lax.axis_size("rep")
    chips = replicas // CORES
    sub = tile // replicas
    rank = lax.axis_index("rep")
    share_rows = local_rows // replicas
    degree_last = filter_weights.shape[0] - 1
    chip, core = rank // CORES, rank % CORES
    places = [
        ((chip + hops) % chips * CORES + core, (chip + hops) % chips * CORES + 1 - core)
        for hops in range(chips)
    ]
    scalars = jnp.stack([tile_counts[0, 0], chip, core, *sum(places, ())]).astype(jnp.int32)

    def along(x, hops):
        step = CORES * hops
        return lax.ppermute(x, "rep", [((i + step) % replicas, i) for i in range(replicas)])

    def partner(x):
        return lax.ppermute(x, "rep", [(i, i ^ 1) for i in range(replicas)])

    def gather(sent):
        half = sent.shape[0] // 2
        before, after, other = along(sent, -1), along(sent, 1), partner(sent)
        live, fetched = load_live(values, scalars, sent, replicas)
        first, second = along(before[:half], -1), along(after[half:], 1)
        crossed = [partner(before), partner(after)]
        crossed += [partner(first), partner(second)]

        def put(fetched, array, hops, other_core, start):
            place = places[hops][other_core]
            return lax.dynamic_update_slice(
                fetched, array[None], (place, start, 0, 0), allow_negative_indices=False
            )

        fetched = put(fetched, other, 0, 1, 0)
        for array, across, hops, start in zip(
            (before, after, first, second), crossed, (-1, 1, 2, 2), (0, 0, 0, half)
        ):
            fetched = put(fetched, array, hops, 0, start)
            fetched = put(fetched, across, hops, 1, start)
        return fetched, live

    def swap(held):
        parts = jnp.stack(held, 1).reshape(replicas, -1, len(held), sub, width)
        parts = lax.all_to_all(parts, "rep", split_axis=0, concat_axis=0, tiled=True)
        parts = parts.transpose(2, 1, 0, 3, 4).reshape(len(held), share_rows, width)
        return [parts[k] for k in range(len(held))]

    def reduce(peer, mine):
        sums = mine + partner(peer).astype(jnp.float32)
        sent = [sums[hops].astype(jnp.bfloat16) for hops in range(chips)]
        half = row_blocks // 2
        low, high = along(sent[2][:half], -1), along(sent[2][half:], 1)
        parts = [along(sent[1], -1), along(sent[3], 1)]
        parts.append(jnp.concatenate([along(low, -1), along(high, 1)], 0))
        total = sums[0]
        for part in parts:
            total = total + part.astype(jnp.float32)
        return total

    served = lax.all_to_all(wanted, "rows", split_axis=0, concat_axis=0, tiled=True)
    blocks = features.reshape(row_blocks, tile, width)
    terms = [lax.dynamic_slice_in_dim(blocks, rank * sub, sub, 1)]
    own = [lax.dynamic_slice_in_dim(features, rank * share_rows, share_rows, 0)]

    def step(degree):
        last = degree == degree_last
        if last:
            own.extend(swap(terms[1:]))
        sent = lax.all_to_all(
            terms[-1][served], "rows", split_axis=0, concat_axis=0, tiled=True
        ).reshape(-1, sub, width)
        fetched, live = gather(sent)
        peer, mine = tile_sums(
            fetched, live, rows_of, slots_of, scalars, row_blocks, whole_blocks=last
        )
        total = reduce(peer, mine)
        if last:
            total = total.reshape(share_rows, width)
            before = own[-2]
        else:
            before = terms[-2] if degree > 1 else None
        following = total if degree == 1 else 2.0 * total - before.astype(jnp.float32)
        (own if last else terms).append(following.astype(jnp.bfloat16))

    for degree in range(1, degree_last + 1):
        step(degree)
    output = jnp.zeros((share_rows, filter_weights.shape[2]), jnp.float32)
    for degree in range(degree_last + 1):
        output = output + jnp.dot(
            own[degree], filter_weights[degree], preferred_element_type=jnp.float32
        )
    return output.astype(jnp.bfloat16)


def solution(mesh):
    return jax.shard_map(
        on_device,
        mesh=mesh,
        in_specs=(
            P("rows", None),
            P("rows", "rep", None, None, None),
            P("rows", "rep", None),
            P("rows", "rep", None),
            P("rows", "rep"),
            P("rows", None, None),
            P(),
        ),
        out_specs=P(("rows", "rep"), None),
        check_vma=False,
    )
```

```python
import jax
import jax.numpy as jnp
from jax import lax
from jax.experimental import pallas as pl
from jax.experimental.pallas import tpu as pltpu
from jax.sharding import PartitionSpec as P


UNROLL = 32
CORES = 2
KEPT = 352


def tile_sums(fetched, values, rows_of, slots_of, scalars, row_blocks, whole_blocks):
    replicas, _, sub, width = fetched.shape
    tile = values.shape[1]
    chips = replicas // CORES
    per = row_blocks // replicas

    def body(scalar, rows, slot, fetched, vals, peer, mine, acc):
        chip = scalar[1]
        core = scalar[2]

        def clear(block, carry):
            acc[block] = jnp.zeros((tile, width), jnp.float32)
            return carry

        lax.fori_loop(0, row_blocks + 1, clear, 0)

        def groups(first, count):
            def group(step, carry):
                products = []
                for unit in range(UNROLL):
                    t = step * UNROLL + unit
                    block = fetched[:, slot[t]].reshape(tile, width)
                    target = jnp.where(t < count, rows[t], row_blocks)
                    products.append(
                        (target, jnp.dot(vals[t], block, preferred_element_type=jnp.float32))
                    )
                for target, product in products:
                    acc[target] += product
                return carry

            lax.fori_loop(first // UNROLL, (count + UNROLL - 1) // UNROLL, group, 0)

        groups(0, jnp.minimum(scalar[0], KEPT))
        groups(KEPT, scalar[-1 + scalar.shape[0]])

        for hops in range(chips):
            for out, from_core in ((peer, 1 - core), (mine, core)):
                rank = lax.rem(chip + hops, chips) * CORES + from_core
                if whole_blocks:
                    share = acc[pl.ds(rank * per, per)].reshape(per * replicas, sub, width)
                else:
                    share = acc[pl.ds(0, row_blocks), pl.ds(pl.multiple_of(rank * sub, sub), sub), :]
                out[hops] = share.astype(out.dtype)

    smem = pl.BlockSpec(memory_space=pltpu.SMEM)
    vmem = pl.BlockSpec(memory_space=pltpu.VMEM)
    shape = (chips, row_blocks, sub, width)
    return pl.pallas_call(
        body,
        out_shape=(
            pltpu.VMEM(shape, jnp.bfloat16),
            pltpu.VMEM(shape, jnp.float32),
        ),
        in_specs=[smem, smem, smem, vmem, vmem],
        out_specs=(vmem, vmem),
        scratch_shapes=[pltpu.VMEM((row_blocks + 1, tile, width), jnp.float32)],
        compiler_params=pltpu.CompilerParams(vmem_limit_bytes=16 * 2**20),
        name="tile_sums",
    )(
        scalars,
        rows_of,
        slots_of,
        pltpu.with_memory_space_constraint(fetched, pltpu.VMEM),
        pltpu.with_memory_space_constraint(values, pltpu.VMEM),
    )


def load_live(values, tail, scalars, sent, replicas):
    def body(scalar, values, tail, sent, live, fetched, semaphore):
        own = (jnp.minimum(scalar[0], KEPT) + UNROLL - 1) // UNROLL
        kept = KEPT // UNROLL
        end = (scalar[-1 + scalar.shape[0]] + UNROLL - 1) // UNROLL

        def copy(source, step, skipped):
            return pltpu.make_async_copy(
                source.at[pl.ds((step - skipped) * UNROLL, UNROLL)],
                live.at[pl.ds(step * UNROLL, UNROLL)],
                semaphore.at[step],
            )

        def start_own(step, carry):
            copy(values, step, 0).start()
            return carry

        def start_tail(step, carry):
            copy(tail, step, kept).start()
            return carry

        def wait_own(step, carry):
            copy(values, step, 0).wait()
            return carry

        def wait_tail(step, carry):
            copy(tail, step, kept).wait()
            return carry

        lax.fori_loop(0, own, start_own, 0)
        lax.fori_loop(kept, end, start_tail, 0)
        fetched[pl.ds(scalar[3], 1)] = sent[...][None]
        lax.fori_loop(0, own, wait_own, 0)
        lax.fori_loop(kept, end, wait_tail, 0)

    return pl.pallas_call(
        body,
        out_shape=(
            pltpu.VMEM(values.shape, values.dtype),
            pltpu.VMEM((replicas, *sent.shape), sent.dtype),
        ),
        in_specs=[
            pl.BlockSpec(memory_space=pltpu.SMEM),
            pl.BlockSpec(memory_space=pltpu.HBM),
            pl.BlockSpec(memory_space=pltpu.HBM),
            pl.BlockSpec(memory_space=pltpu.VMEM),
        ],
        out_specs=(
            pl.BlockSpec(memory_space=pltpu.VMEM),
            pl.BlockSpec(memory_space=pltpu.VMEM),
        ),
        scratch_shapes=[pltpu.SemaphoreType.DMA((values.shape[0] // UNROLL,))],
        compiler_params=pltpu.CompilerParams(vmem_limit_bytes=2 * 2**20),
        name="load_live",
    )(
        scalars,
        pltpu.with_memory_space_constraint(values, pltpu.HBM),
        pltpu.with_memory_space_constraint(tail, pltpu.HBM),
        pltpu.with_memory_space_constraint(sent, pltpu.VMEM),
    )


def on_device(
    features, tile_values, tile_rows, tile_slots, tile_counts, fetch_lists, filter_weights
):
    values = tile_values[0, 0]
    rows_of = tile_rows[0, 0]
    slots_of = tile_slots[0, 0]
    wanted = fetch_lists[0]
    tile = values.shape[1]
    local_rows, width = features.shape
    row_blocks = local_rows // tile
    replicas = lax.axis_size("rep")
    chips = replicas // CORES
    sub = tile // replicas
    rank = lax.axis_index("rep")
    share_rows = local_rows // replicas
    degree_last = filter_weights.shape[0] - 1
    chip, core = rank // CORES, rank % CORES
    places = [
        ((chip + hops) % chips * CORES + core, (chip + hops) % chips * CORES + 1 - core)
        for hops in range(chips)
    ]

    def along(x, hops):
        step = CORES * hops
        return lax.ppermute(x, "rep", [((i + step) % replicas, i) for i in range(replicas)])

    def partner(x):
        return lax.ppermute(x, "rep", [(i, i ^ 1) for i in range(replicas)])

    count = tile_counts[0, 0]
    tail = partner(values[KEPT:])
    given = jnp.concatenate([rows_of[KEPT:], slots_of[KEPT:], tile_counts[0]])
    taken = partner(given)
    past = values.shape[0] - KEPT
    rows_of = jnp.concatenate([rows_of[:KEPT], taken[:past]])
    slots_of = jnp.concatenate([slots_of[:KEPT], taken[past : 2 * past]])
    scalars = jnp.stack([count, chip, core, *sum(places, ()), taken[2 * past]]).astype(jnp.int32)

    def gather(sent):
        half = sent.shape[0] // 2
        before, after, other = along(sent, -1), along(sent, 1), partner(sent)
        live, fetched = load_live(values, tail, scalars, sent, replicas)
        first, second = along(before[:half], -1), along(after[half:], 1)
        crossed = [partner(before), partner(after)]
        crossed += [partner(first), partner(second)]

        def put(fetched, array, hops, other_core, start):
            place = places[hops][other_core]
            return lax.dynamic_update_slice(
                fetched, array[None], (place, start, 0, 0), allow_negative_indices=False
            )

        fetched = put(fetched, other, 0, 1, 0)
        for array, across, hops, start in zip(
            (before, after, first, second), crossed, (-1, 1, 2, 2), (0, 0, 0, half)
        ):
            fetched = put(fetched, array, hops, 0, start)
            fetched = put(fetched, across, hops, 1, start)
        return fetched, live

    def swap(held):
        parts = jnp.stack(held, 1).reshape(replicas, -1, len(held), sub, width)
        parts = lax.all_to_all(parts, "rep", split_axis=0, concat_axis=0, tiled=True)
        parts = parts.transpose(2, 1, 0, 3, 4).reshape(len(held), share_rows, width)
        return [parts[k] for k in range(len(held))]

    def reduce(peer, mine):
        sums = mine + partner(peer).astype(jnp.float32)
        total = sums[0]
        for hops in range(1, chips):
            total = total + along(sums[hops].astype(jnp.bfloat16), -hops).astype(jnp.float32)
        return total

    served = lax.all_to_all(wanted, "rows", split_axis=0, concat_axis=0, tiled=True)
    blocks = features.reshape(row_blocks, tile, width)
    terms = [lax.dynamic_slice_in_dim(blocks, rank * sub, sub, 1)]
    own = [lax.dynamic_slice_in_dim(features, rank * share_rows, share_rows, 0)]

    def step(degree):
        last = degree == degree_last
        if last:
            own.extend(swap(terms[1:]))
        sent = lax.all_to_all(
            terms[-1][served], "rows", split_axis=0, concat_axis=0, tiled=True
        ).reshape(-1, sub, width)
        fetched, live = gather(sent)
        peer, mine = tile_sums(
            fetched, live, rows_of, slots_of, scalars, row_blocks, whole_blocks=last
        )
        total = reduce(peer, mine)
        if last:
            total = total.reshape(share_rows, width)
            before = own[-2]
        else:
            before = terms[-2] if degree > 1 else None
        following = total if degree == 1 else 2.0 * total - before.astype(jnp.float32)
        (own if last else terms).append(following.astype(jnp.bfloat16))

    for degree in range(1, degree_last + 1):
        step(degree)
    output = jnp.zeros((share_rows, filter_weights.shape[2]), jnp.float32)
    for degree in range(degree_last + 1):
        output = output + jnp.dot(
            own[degree], filter_weights[degree], preferred_element_type=jnp.float32
        )
    return output.astype(jnp.bfloat16)


def solution(mesh):
    return jax.shard_map(
        on_device,
        mesh=mesh,
        in_specs=(
            P("rows", None),
            P("rows", "rep", None, None, None),
            P("rows", "rep", None),
            P("rows", "rep", None),
            P("rows", "rep"),
            P("rows", None, None),
            P(),
        ),
        out_specs=P(("rows", "rep"), None),
        check_vma=False,
    )
```

```python
import jax
import jax.numpy as jnp
from jax import lax
from jax.experimental import pallas as pl
from jax.experimental.pallas import tpu as pltpu
from jax.sharding import PartitionSpec as P


UNROLL = 32
CORES = 2


def tile_sums(fetched, values, rows_of, slots_of, scalars, row_blocks, whole_blocks):
    replicas, _, sub, width = fetched.shape
    tile = values.shape[1]
    chips = replicas // CORES
    per = row_blocks // replicas

    def body(scalar, rows, slot, fetched, vals, peer, mine, acc):
        count = scalar[0]
        chip = scalar[1]
        core = scalar[2]

        def clear(block, carry):
            acc[block] = jnp.zeros((tile, width), jnp.float32)
            return carry

        lax.fori_loop(0, row_blocks + 1, clear, 0)

        def group(step, carry):
            products = []
            for unit in range(UNROLL):
                t = step * UNROLL + unit
                block = fetched[:, slot[t]].reshape(tile, width)
                target = jnp.where(t < count, rows[t], row_blocks)
                products.append(
                    (target, jnp.dot(vals[t], block, preferred_element_type=jnp.float32))
                )
            for target, product in products:
                acc[target] += product
            return carry

        lax.fori_loop(0, (count + UNROLL - 1) // UNROLL, group, 0)

        for hops in range(chips):
            for out, from_core in ((peer, 1 - core), (mine, core)):
                rank = lax.rem(chip + hops, chips) * CORES + from_core
                if whole_blocks:
                    share = acc[pl.ds(rank * per, per)].reshape(per * replicas, sub, width)
                else:
                    share = acc[pl.ds(0, row_blocks), pl.ds(pl.multiple_of(rank * sub, sub), sub), :]
                out[hops] = share.astype(out.dtype)

    smem = pl.BlockSpec(memory_space=pltpu.SMEM)
    vmem = pl.BlockSpec(memory_space=pltpu.VMEM)
    shape = (chips, row_blocks, sub, width)
    return pl.pallas_call(
        body,
        out_shape=(
            pltpu.VMEM(shape, jnp.bfloat16),
            pltpu.VMEM(shape, jnp.float32),
        ),
        in_specs=[smem, smem, smem, vmem, vmem],
        out_specs=(vmem, vmem),
        scratch_shapes=[pltpu.VMEM((row_blocks + 1, tile, width), jnp.float32)],
        compiler_params=pltpu.CompilerParams(vmem_limit_bytes=16 * 2**20),
        name="tile_sums",
    )(
        scalars,
        rows_of,
        slots_of,
        pltpu.with_memory_space_constraint(fetched, pltpu.VMEM),
        pltpu.with_memory_space_constraint(values, pltpu.VMEM),
    )


def load_live(values, scalars, sent, replicas):
    def body(scalar, values, sent, live, fetched, semaphore):
        groups = (scalar[0] + UNROLL - 1) // UNROLL

        def copy(step):
            part = pl.ds(step * UNROLL, UNROLL)
            return pltpu.make_async_copy(values.at[part], live.at[part], semaphore.at[step])

        def start(step, carry):
            copy(step).start()
            return carry

        def wait(step, carry):
            copy(step).wait()
            return carry

        lax.fori_loop(0, groups, start, 0)
        fetched[pl.ds(scalar[3], 1)] = sent[...][None]
        lax.fori_loop(0, groups, wait, 0)

    return pl.pallas_call(
        body,
        out_shape=(
            pltpu.VMEM(values.shape, values.dtype),
            pltpu.VMEM((replicas, *sent.shape), sent.dtype),
        ),
        in_specs=[
            pl.BlockSpec(memory_space=pltpu.SMEM),
            pl.BlockSpec(memory_space=pltpu.HBM),
            pl.BlockSpec(memory_space=pltpu.VMEM),
        ],
        out_specs=(
            pl.BlockSpec(memory_space=pltpu.VMEM),
            pl.BlockSpec(memory_space=pltpu.VMEM),
        ),
        scratch_shapes=[pltpu.SemaphoreType.DMA((values.shape[0] // UNROLL,))],
        compiler_params=pltpu.CompilerParams(vmem_limit_bytes=2 * 2**20),
        name="load_live",
    )(
        scalars,
        pltpu.with_memory_space_constraint(values, pltpu.HBM),
        pltpu.with_memory_space_constraint(sent, pltpu.VMEM),
    )


def on_device(
    features, tile_values, tile_rows, tile_slots, tile_counts, fetch_lists, filter_weights
):
    values = tile_values[0, 0]
    rows_of = tile_rows[0, 0]
    slots_of = tile_slots[0, 0]
    wanted = fetch_lists[0]
    tile = values.shape[1]
    local_rows, width = features.shape
    row_blocks = local_rows // tile
    replicas = lax.axis_size("rep")
    chips = replicas // CORES
    sub = tile // replicas
    rank = lax.axis_index("rep")
    share_rows = local_rows // replicas
    degree_last = filter_weights.shape[0] - 1
    chip, core = rank // CORES, rank % CORES
    places = [
        ((chip + hops) % chips * CORES + core, (chip + hops) % chips * CORES + 1 - core)
        for hops in range(chips)
    ]
    scalars = jnp.stack([tile_counts[0, 0], chip, core, *sum(places, ())]).astype(jnp.int32)

    def along(x, hops):
        step = CORES * hops
        return lax.ppermute(x, "rep", [((i + step) % replicas, i) for i in range(replicas)])

    def partner(x):
        return lax.ppermute(x, "rep", [(i, i ^ 1) for i in range(replicas)])

    def gather(sent):
        half = sent.shape[0] // 2
        before, after, other = along(sent, -1), along(sent, 1), partner(sent)
        live, fetched = load_live(values, scalars, sent, replicas)
        first, second = along(before[:half], -1), along(after[half:], 1)
        crossed = [partner(before), partner(after)]
        crossed += [partner(first), partner(second)]

        def put(fetched, array, hops, other_core, start):
            place = places[hops][other_core]
            return lax.dynamic_update_slice(
                fetched, array[None], (place, start, 0, 0), allow_negative_indices=False
            )

        fetched = put(fetched, other, 0, 1, 0)
        for array, across, hops, start in zip(
            (before, after, first, second), crossed, (-1, 1, 2, 2), (0, 0, 0, half)
        ):
            fetched = put(fetched, array, hops, 0, start)
            fetched = put(fetched, across, hops, 1, start)
        return fetched, live

    def swap(held):
        parts = jnp.stack(held, 1).reshape(replicas, -1, len(held), sub, width)
        parts = lax.all_to_all(parts, "rep", split_axis=0, concat_axis=0, tiled=True)
        parts = parts.transpose(2, 1, 0, 3, 4).reshape(len(held), share_rows, width)
        return [parts[k] for k in range(len(held))]

    def reduce(peer, mine):
        sums = mine + partner(peer).astype(jnp.float32)
        total = sums[0]
        for hops in range(1, chips):
            total = total + along(sums[hops].astype(jnp.bfloat16), -hops).astype(jnp.float32)
        return total

    served = lax.all_to_all(wanted, "rows", split_axis=0, concat_axis=0, tiled=True)
    blocks = features.reshape(row_blocks, tile, width)
    terms = [lax.dynamic_slice_in_dim(blocks, rank * sub, sub, 1)]
    shares = features.reshape(replicas, share_rows, width)
    own = [lax.dynamic_index_in_dim(shares, rank, 0, keepdims=False, allow_negative_indices=False)]

    def step(degree):
        last = degree == degree_last
        if last:
            own.extend(swap(terms[1:]))
        sent = lax.all_to_all(
            terms[-1][served], "rows", split_axis=0, concat_axis=0, tiled=True
        ).reshape(-1, sub, width)
        fetched, live = gather(sent)
        peer, mine = tile_sums(
            fetched, live, rows_of, slots_of, scalars, row_blocks, whole_blocks=last
        )
        total = reduce(peer, mine)
        if last:
            total = total.reshape(share_rows, width)
            before = own[-2]
        else:
            before = terms[-2] if degree > 1 else None
        following = total if degree == 1 else 2.0 * total - before.astype(jnp.float32)
        (own if last else terms).append(following.astype(jnp.bfloat16))

    for degree in range(1, degree_last + 1):
        step(degree)
    output = jnp.zeros((share_rows, filter_weights.shape[2]), jnp.float32)
    for degree in range(degree_last + 1):
        output = output + jnp.dot(
            own[degree], filter_weights[degree], preferred_element_type=jnp.float32
        )
    return output.astype(jnp.bfloat16)


def solution(mesh):
    return jax.shard_map(
        on_device,
        mesh=mesh,
        in_specs=(
            P("rows", None),
            P("rows", "rep", None, None, None),
            P("rows", "rep", None),
            P("rows", "rep", None),
            P("rows", "rep"),
            P("rows", None, None),
            P(),
        ),
        out_specs=P(("rows", "rep"), None),
        check_vma=False,
    )
```
